32 devices in a mesh: beam: 2 (over y), sub: 8 (over z, x), tm: 2 (over core).
Axes of the slice: x: 2, y: 2, z: 4, core: 2. Of those that a mesh axis runs over, the one named last changes fastest.
Arguments:
- filterbank: bfloat16 [2048, 1024], P(('beam', 'sub'), 'tm'), parts along dimension 0, may hold values from -6 to 6
- bandpass: float32 [2048], P(('beam', 'sub')), parts along dimension 0, may hold values from 0.3 to 3
- local_delays: int32 [7, 1024], P(None, 'sub'), may hold values from 0 to 32, as said below
- cross_delays: int32 [3, 128], P(None, 'sub'), may hold values from 0 to 32, as said below
Outputs:
- dedispersed: float32 [256, 1024], P(('beam', 'sub'), 'tm'), parts along dimension 0
The draws below stay inside these ranges and needn't reach their ends.
There are 2 independent parts, one for each index of `beam`. The reference program is written for one: setup_inputs(seed, part) draws one part's arguments, and reference() takes and returns one part's arrays. A program takes and returns all parts, laid end to end along the dimension named above; an argument that names none is the same for every part. Nothing has to cross between parts.
Inputs may be any that keep to these rules, and one draw needn't show every extreme that they name: `local_delays`: whole samples; level m of the local levels reads its first entries of each block of 128. `cross_delays`: whole samples.
All inputs are finite; a program needn't handle non-finite values.
Results may differ from the reference program's by a relative error of at most 0.0003.
Values may be sent and summed in bfloat16 or wider, within the bound.
A program may use at most 64 MiB of HBM per device.

```python
import math
import jax
import jax.numpy as jnp
from jax import lax

CH_DEV = 128
KD = 16
CHANNELS = 1024
SAMPLES = 1024
TRIALS = 128
LLEV = 7
XLEV = 3
SHIFT_MAX = 32
N_SUB = 8


def draw_local_delays(key, part):
    delays = jax.random.randint(key, (LLEV, CHANNELS), 0, SHIFT_MAX + 1, dtype=jnp.int32)
    return delays.at[0, 0].set(SHIFT_MAX)


def draw_cross_delays(key, part):
    delays = jax.random.randint(jax.random.fold_in(key, 7), (XLEV, TRIALS), 0, SHIFT_MAX + 1, dtype=jnp.int32)
    return delays.at[XLEV - 1, 0].set(SHIFT_MAX)


def level_of(own_key, dims, pieces, least, top_value):
    level, own = 1.0, jax.random.fold_in(own_key, 6)
    for axis_at, parts in pieces:
        draws = jnp.exp(jax.random.uniform(jax.random.fold_in(own, axis_at), (parts,), jnp.float32, least / len(pieces), top_value / len(pieces)))
        level = level * jnp.repeat(draws, dims[axis_at] // parts).reshape([-1 if axis == axis_at else 1 for axis in range(len(dims))])
    return level


def scatter_about(own_key, shape, width, bound, split=(), kind=jnp.bfloat16):
    factor_of = level_of(own_key, shape, split, -0.22, 0.18) if split else 1.0
    array = jax.random.normal(own_key, shape, jnp.float32) * width * factor_of
    return jnp.minimum(jnp.maximum(array, -bound), bound).astype(kind)


def setup_inputs(seed: int = 0, part: int = 0) -> dict:
    streams_of = jax.random.split(jax.random.key(seed), 5)
    own_keys = jax.random.split(jax.random.fold_in(streams_of[4], part), 5)
    filterbank = scatter_about(own_keys[0], (CHANNELS, SAMPLES), 1.0, 6.0, ((0, 8), (1, 2)))
    bandpass = jnp.clip(jnp.exp(math.log(3.0) - 2.3025851 * jax.random.uniform(own_keys[1], (CHANNELS,), jnp.float32) ** level_of(own_keys[1], (CHANNELS,), ((0, 8),), -0.2, 0.2)), 0.3, 3.0)
    local_delays = draw_local_delays(jax.random.fold_in(streams_of[4], 71), part)
    cross_delays = draw_cross_delays(jax.random.fold_in(streams_of[4], 71), part)
    return dict(filterbank=filterbank, bandpass=bandpass, local_delays=local_delays, cross_delays=cross_delays)


def delayed(upper, delays):
    padded = jnp.pad(upper, ((0, 0), (SHIFT_MAX, 0)))
    columns = lax.broadcasted_iota(jnp.int32, upper.shape, 1)
    offsets = columns + SHIFT_MAX - delays[:, None].astype(jnp.int32)
    return jnp.take_along_axis(padded, offsets, axis=1)

def reference(filterbank, bandpass, local_delays, cross_delays):
    corrected = filterbank.astype(jnp.float32) * bandpass[:, None]
    padded = jnp.pad(corrected, ((0, 0), (15, 15)))
    window_total = lax.reduce_window(padded, jnp.zeros((), padded.dtype), lax.add, (1, 31), (1, 1), 'VALID')
    current = corrected - window_total / 31.0
    trial_count = 1
    for level_index in range(LLEV):
        band_count = current.shape[0] // trial_count
        grouped = current.reshape(band_count // 2, 2, trial_count, SAMPLES)
        lower = grouped[:, 0]
        upper = grouped[:, 1]
        new_count = min(2 * trial_count, KD)
        if new_count > trial_count:
            lower = jnp.concatenate([lower, lower], axis=1)
            upper = jnp.concatenate([upper, upper], axis=1)
        per_device = band_count // 2 // N_SUB * new_count
        delays = local_delays[level_index].reshape(N_SUB, CH_DEV)[:, :per_device].reshape(-1)
        current = lower.reshape(-1, SAMPLES) + delayed(upper.reshape(-1, SAMPLES), delays)
        trial_count = new_count
    for level_index in range(XLEV):
        grouped = current.reshape(-1, 2, trial_count, SAMPLES)
        lower = jnp.concatenate([grouped[:, 0], grouped[:, 0]], axis=1)
        upper = jnp.concatenate([grouped[:, 1], grouped[:, 1]], axis=1)
        current = lower.reshape(-1, SAMPLES) + delayed(upper.reshape(-1, SAMPLES), cross_delays[level_index])
        trial_count = 2 * trial_count
    return current * (1.0 / math.sqrt(CHANNELS))
```

```python
import functools
import math

import jax
import jax.numpy as jnp
from jax import lax
from jax.experimental import pallas as pl
from jax.experimental.pallas import tpu as pltpu
from jax.sharding import PartitionSpec as P

MESH = pl.DeviceIdType.MESH
LANES = 128
SUB = 8
HALF = 15
WINDOW = 31.0
HEADER = 32
RADIX_LEVELS = 3
TOP = 32767.0
ROUNDER = 12582912.0
TINY = 1e-30


def tiles_of(columns):
    return -(-columns // LANES)


def delayed(tiles, delay, lane, count):
    tiles = tiles[max(0, len(tiles) - count - 1) :]
    source = (lane - delay) & (LANES - 1)
    keep = lane >= delay
    turned = [jnp.take_along_axis(t, source, axis=1, mode="promise_in_bounds") for t in tiles]
    if len(turned) == count:
        turned = [jnp.zeros_like(turned[0])] + turned
    return [jnp.where(keep, turned[k + 1], turned[k]) for k in range(count)]


def merged_right(lower, upper, delay, lane, count):
    source = (lane - delay) & (LANES - 1)
    keep = lane >= delay
    turned = [jnp.take_along_axis(t, source, axis=1, mode="promise_in_bounds") for t in upper]
    zero = jnp.zeros_like(turned[0])
    made = []
    for k in range(count):
        here = turned[k] if k < len(turned) else zero
        left = turned[k - 1] if k else zero
        moved = jnp.where(keep, here, left)
        made.append(lower[k] + moved if k < len(lower) else moved)
    return made


def paired(mine, theirs, on_top, delay, lane, count):
    lower = [jnp.where(on_top, t, m) for t, m in zip(theirs, mine)]
    upper = [jnp.where(on_top, m, t) for t, m in zip(theirs, mine)]
    moved = delayed(upper, delay, lane, count)
    return [a + b for a, b in zip(lower[len(lower) - count :], moved)]


def phases_of(cross_levels):
    phases = []
    for level in range(0, cross_levels, RADIX_LEVELS):
        depth = min(RADIX_LEVELS, cross_levels - level)
        phases.append((level, depth, [m << level for m in range(1, 1 << depth)]))
    return phases


def coded(x, inverse):
    return jnp.clip(x * inverse + ROUNDER - ROUNDER, -TOP, TOP)


def scales_of(peaks):
    exponents = []
    for peak in peaks:
        top = jnp.maximum(jnp.max(peak, axis=1, keepdims=True), TINY)
        exponent = jnp.floor(jnp.log2(top) + 0.001) - 14.0
        exponents.append(jnp.broadcast_to(exponent, (SUB, LANES)))
    return exponents, [jnp.exp2(-e) for e in exponents]


def peaks_of(rows):
    return [functools.reduce(jnp.maximum, [jnp.abs(t) for t in tiles]) for tiles in rows]


def kernel(
    geometry,
    fb_hbm, bp_hbm, ld_hbm, cd_hbm,
    out_ref,
    fpad, bp_v, ld_v, cd_v, x0, delay_l, cd_far, plane, edge_sent, edge_got, sent, got,
    load_sem, edge_send, edge_recv, far_send, far_recv, cross_send, cross_recv,
):
    channels, span, local_levels, cross_levels, trials, shift_max, norm = geometry
    own = span // LANES
    before = tiles_of(cross_levels * shift_max + HEADER)
    width = before + own
    growth = trials.bit_length() - 1
    row_tiles = trials // SUB
    tm = lax.axis_index("tm")
    sub = lax.axis_index("sub")
    other = 1 - tm
    phases = phases_of(cross_levels)
    edge_masks = [0] + phases[0][2]

    barrier = pltpu.get_barrier_semaphore()
    partners = 0
    for mask in edge_masks:
        target = {"sub": sub ^ mask, "tm": other} if mask else {"tm": other}
        pl.semaphore_signal(barrier, inc=1, device_id=target, device_id_type=MESH)
        partners += 1
    for level, depth, masks in phases:
        for mask in masks:
            pl.semaphore_signal(barrier, inc=1, device_id={"sub": sub ^ mask}, device_id_type=MESH)
            partners += 1

    counts = [tiles_of(span + HALF + (m + 1) * shift_max) for m in range(local_levels)]
    start = own + 1
    loads = [
        pltpu.make_async_copy(ld_hbm, ld_v, load_sem.at[0]),
        pltpu.make_async_copy(cd_hbm, cd_v, load_sem.at[1]),
        pltpu.make_async_copy(bp_hbm, bp_v, load_sem.at[2]),
        pltpu.make_async_copy(
            fb_hbm, fpad.at[:, pl.ds(pl.multiple_of(tm * LANES, LANES), span)], load_sem.at[3]
        ),
    ]
    for load in loads:
        load.start()

    edge_tiles = counts[-1] - own + before

    @pl.when(tm == 0)
    def _():
        fpad[:, span : start * LANES] = jnp.zeros((channels, LANES), fpad.dtype)
        for slot in range(len(edge_masks)):
            edge_got[slot, :, : edge_tiles * LANES] = jnp.zeros((trials, edge_tiles * LANES), edge_got.dtype)

    @pl.when(tm == 1)
    def _():
        fpad[:, :LANES] = jnp.zeros((channels, LANES), fpad.dtype)
        for slot in range(len(edge_masks)):
            edge_got[slot, :, edge_tiles * LANES :] = jnp.zeros((trials, LANES), edge_got.dtype)

    for load in loads[:3]:
        load.wait()
    ones = jnp.ones((channels, LANES), jnp.float32).astype(jnp.bfloat16)
    row_at = lax.broadcasted_iota(jnp.int32, (channels, channels), 0)
    col_at = lax.broadcasted_iota(jnp.int32, (channels, channels), 1)
    diagonal = row_at == col_at
    rows = channels
    for level in range(local_levels):
        if level >= growth:
            rows //= 2
        spread = jnp.where(diagonal[:rows], ld_v[level : level + 1, :].astype(jnp.float32), 0.0)
        spread = jnp.dot(spread.astype(jnp.bfloat16), ones, preferred_element_type=jnp.float32)
        delay_l[level, :rows, :] = spread.astype(jnp.int32)

    def spread_of(delays):
        spread = jnp.where(diagonal[:trials, :trials], delays.astype(jnp.float32), 0.0)
        spread = jnp.dot(spread.astype(jnp.bfloat16), ones[:trials], preferred_element_type=jnp.float32)
        return spread.astype(jnp.int32)

    delay_c = [spread_of(cd_v[level : level + 1, :]) for level in range(cross_levels)]
    gain = jnp.dot(
        jnp.where(diagonal, bp_v[...], 0.0), jnp.ones((channels, LANES), jnp.float32),
        precision=lax.Precision.HIGHEST, preferred_element_type=jnp.float32,
    )
    band_row = lax.broadcasted_iota(jnp.int32, (3 * LANES, LANES), 0)
    band_col = lax.broadcasted_iota(jnp.int32, (3 * LANES, LANES), 1)
    apart = band_row - LANES - band_col
    band = jnp.where((apart >= -HALF) & (apart <= HALF), 1.0, 0.0).astype(jnp.bfloat16)

    loads[3].wait()
    for k in range(start):
        low, high = max(k - 1, 0), min(k + 2, start)
        total = jnp.dot(
            fpad[:, low * LANES : high * LANES], band[(low - k + 1) * LANES : (high - k + 1) * LANES],
            preferred_element_type=jnp.float32,
        )
        centre = fpad[:, k * LANES : (k + 1) * LANES].astype(jnp.float32)
        x0[:, k * LANES : (k + 1) * LANES] = gain * (centre - total / WINDOW)

    lane = lax.broadcasted_iota(jnp.int32, (SUB, LANES), 1)
    sublane = lax.broadcasted_iota(jnp.int32, (SUB, LANES), 0)

    def block(at, carry):
        base = at * trials
        current = []
        for r in range(row_tiles):
            here = pl.ds(pl.multiple_of(base + r * SUB, SUB), SUB)
            current.append([x0[here, k * LANES : (k + 1) * LANES] for k in range(start)])
        for level in range(growth):
            count, step = counts[level], 1 << level
            following = []
            for r in range(row_tiles):
                delay = delay_l[level, pl.ds(pl.multiple_of(base + r * SUB, SUB), SUB), :]
                if step < SUB:
                    is_upper = (sublane & step) != 0
                    lower, upper = [], []
                    for t in current[r]:
                        down = pltpu.roll(t, step, 0)
                        up = down if 2 * step == SUB else pltpu.roll(t, SUB - step, 0)
                        lower.append(jnp.where(is_upper, down, t))
                        upper.append(jnp.where(is_upper, t, up))
                else:
                    apart = step // SUB
                    lower, upper = current[r & ~apart], current[r | apart]
                following.append(merged_right(lower, upper, delay, lane, count))
            current = following
        for r in range(row_tiles):
            here = pl.ds(pl.multiple_of(base + r * SUB, SUB), SUB)
            for k, t in enumerate(current[r]):
                plane[here, k * LANES : (k + 1) * LANES] = t
        return carry

    lax.fori_loop(0, channels // trials, block, 0, unroll=True)

    bands = channels // trials
    count = counts[growth - 1]
    current = [
        [[plane[(b * row_tiles + r) * SUB : (b * row_tiles + r + 1) * SUB, k * LANES : (k + 1) * LANES] for k in range(count)] for r in range(row_tiles)]
        for b in range(bands)
    ]
    for level in range(growth, local_levels):
        count = counts[level]
        bands //= 2
        following = []
        for b in range(bands):
            made = []
            for r in range(row_tiles):
                at = (b * row_tiles + r) * SUB
                delay = delay_l[level, at : at + SUB, :]
                made.append(merged_right(current[2 * b][r], current[2 * b + 1][r], delay, lane, count))
            following.append(made)
        current = following
    frame = current[0]


    rows_of = []
    for r in range(row_tiles):
        tiles = []
        for t in range(-before, own):
            zero = jnp.zeros_like(frame[r][0])
            early = frame[r][t] if t >= 0 else zero
            late = frame[r][t + 1] if t >= -1 else zero
            tiles.append(jnp.where(tm == 1, late, early))
        rows_of.append(tiles)

    wide_lane = lax.broadcasted_iota(jnp.int32, (trials, LANES), 1)
    is_header = wide_lane < HEADER

    def fill(ref, k, tiles, inverses, header):
        if tiles is None:
            tile = header
        else:
            tile = jnp.concatenate([coded(t, i) for t, i in zip(tiles, inverses)], axis=0)
            if header is not None:
                tile = jnp.where(is_header, header, tile)
        ref[:, k * LANES : (k + 1) * LANES] = tile.astype(jnp.int32).astype(jnp.int16)

    def prepare(at, rows, exponents, inverses):
        header = jnp.concatenate(exponents, axis=0)
        skip = width - len(rows[0])
        for k in range(width):
            if k == 0 or k >= skip:
                fill(sent.at[at], k, [p[k - skip] for p in rows] if k >= skip else None, inverses, None if k else header)

    def plane_copy(at, index, mask):
        return pltpu.make_async_remote_copy(
            src_ref=sent.at[at], dst_ref=got.at[at, index],
            send_sem=cross_send.at[at, index], recv_sem=cross_recv.at[at, index],
            device_id={"sub": sub ^ mask}, device_id_type=MESH,
        )

    def edge_pair(slot, mask):
        target = {"sub": sub ^ mask, "tm": other} if mask else {"tm": other}
        onward = pltpu.make_async_remote_copy(
            src_ref=edge_sent, dst_ref=edge_got.at[slot, :, pl.ds(0, edge_tiles * LANES)],
            send_sem=edge_send.at[slot], recv_sem=edge_recv.at[slot],
            device_id=target, device_id_type=MESH,
        )
        backward = pltpu.make_async_remote_copy(
            src_ref=edge_sent.at[:, pl.ds(0, LANES)], dst_ref=edge_got.at[slot, :, pl.ds(edge_tiles * LANES, LANES)],
            send_sem=edge_send.at[slot], recv_sem=edge_recv.at[slot],
            device_id=target, device_id_type=MESH,
        )
        return onward, backward

    far_copies = {}
    for level, depth, masks in phases:
        for mask in masks[1::2]:
            index = len(far_copies)
            far_copies[mask] = pltpu.make_async_remote_copy(
                src_ref=cd_v, dst_ref=cd_far.at[index],
                send_sem=far_send.at[index], recv_sem=far_recv.at[index],
                device_id={"sub": sub ^ mask}, device_id_type=MESH,
            )
    far_at = {mask: index for index, mask in enumerate(far_copies)}
    plane_copies = [[plane_copy(at, index, mask) for index, mask in enumerate(masks)] for at, (_, _, masks) in enumerate(phases)]
    edge_copies = [edge_pair(slot, mask) for slot, mask in enumerate(edge_masks)]

    exponents, inverses = scales_of(peaks_of(frame))
    prepare(0, rows_of, exponents, inverses)
    header = jnp.concatenate(exponents, axis=0)
    for k in range(edge_tiles):
        onward = [frame[r][own - before + k] for r in range(row_tiles)]
        if k == 0:
            onward = [jnp.where(tm == 1, frame[r][0], onward[r]) for r in range(row_tiles)]
        fill(edge_sent, k, onward, inverses, None if k else header)

    pl.semaphore_wait(barrier, partners)

    for slot in range(len(edge_masks) - 1, -1, -1):
        if slot:
            plane_copies[0][slot - 1].start()

        @pl.when(tm == 0)
        def _():
            edge_copies[slot][0].start()

        @pl.when(tm == 1)
        def _():
            edge_copies[slot][1].start()

    for copy in far_copies.values():
        copy.start()

    def decoded(tile):
        return tile.astype(jnp.int32).astype(jnp.float32)

    def split(tile):
        return [tile[r * SUB : (r + 1) * SUB] for r in range(row_tiles)]

    def scale_from(header):
        return jnp.exp2(jnp.broadcast_to(header[:, :1], (trials, LANES)))

    def with_edge(slot, rows):
        onward, backward = edge_copies[slot]

        @pl.when(tm == 0)
        def _():
            backward.wait_recv()

        @pl.when(tm == 1)
        def _():
            onward.wait_recv()

        tiles = [decoded(edge_got[slot, :, k * LANES : (k + 1) * LANES]) for k in range(edge_tiles + 1)]
        scale = scale_from(jnp.where(tm == 1, tiles[0], tiles[-1]))
        tiles[-1] = jnp.where(is_header, 0.0, tiles[-1])
        made = [list(row) for row in rows]
        for at, tile in zip(list(range(edge_tiles)) + [width - 1], tiles):
            for r, part in enumerate(split(tile * scale)):
                made[r][at] = made[r][at] + part
        return made

    def landed(at, mask, count):
        index = phases[at][2].index(mask)
        plane_copies[at][index].wait_recv()
        tiles = [decoded(got[at, index, :, k * LANES : (k + 1) * LANES]) for k in [0] + list(range(max(width - count, 1), width))]
        scale = scale_from(tiles[0])
        tiles = tiles[1:] if count < width else tiles
        parts = [split(t * scale) for t in tiles]
        rows = [[p[r] for p in parts] for r in range(row_tiles)]
        return rows if at else with_edge(index + 1, rows)

    def merged(at, mask, depth):
        level = phases[at][0]
        if depth == 0:
            return landed(at, mask, len(rows_of[0])) if mask else rows_of
        step = level + depth - 1
        mine = merged(at, mask, depth - 1)
        theirs = merged(at, mask | (1 << step), depth - 1)
        delay = delay_c[step] if mask == 0 else spread_of(cd_far[far_at[mask], step : step + 1, :])
        count = own + tiles_of((cross_levels - step - 1) * shift_max)
        on_top = (sub >> step) & 1 == 1
        return [paired(mine[r], theirs[r], on_top, delay[r * SUB : (r + 1) * SUB], lane, count) for r in range(row_tiles)]

    rows_of = with_edge(0, rows_of)
    for at, (level, depth, masks) in enumerate(phases):
        if at:
            prepare(at, rows_of, *scales_of(peaks_of(rows_of)))
            for copy in reversed(plane_copies[at]):
                copy.start()
        for mask in masks[1::2]:
            far_copies[mask].wait_recv()
        rows_of = merged(at, 0, depth)

    for r in range(row_tiles):
        for k, t in enumerate(rows_of[r][-own:]):
            out_ref[r * SUB : (r + 1) * SUB, k * LANES : (k + 1) * LANES] = t * norm
    for copy in [c for row in plane_copies for c in row] + list(far_copies.values()):
        copy.wait_send()

    @pl.when(tm == 0)
    def _():
        for onward, backward in edge_copies:
            onward.wait_send()

    @pl.when(tm == 1)
    def _():
        for onward, backward in edge_copies:
            backward.wait_send()


def shards(filterbank, bandpass, local_delays, cross_delays):
    channels, span = filterbank.shape
    shift_max = span // 16
    local_levels = local_delays.shape[0]
    cross_levels = lax.axis_size("sub").bit_length() - 1
    trials = cross_delays.shape[1]
    norm = 1.0 / math.sqrt(channels * lax.axis_size("sub"))
    own = span // LANES
    before = tiles_of(cross_levels * shift_max + HEADER)
    width = (own + before) * LANES
    frame = tiles_of(span + HALF + local_levels * shift_max)
    edges = (frame - own + before) * LANES
    phases = phases_of(cross_levels)
    most = len(phases[0][2])
    far = max(sum(len(masks[1::2]) for _, _, masks in phases), 1)
    geometry = (channels, span, local_levels, cross_levels, trials, shift_max, norm)
    return pl.pallas_call(
        functools.partial(kernel, geometry),
        out_shape=pltpu.VMEM((trials, span), jnp.float32),
        in_specs=[pl.BlockSpec(memory_space=pl.ANY)] * 4,
        out_specs=pl.BlockSpec(memory_space=pltpu.VMEM),
        scratch_shapes=[
            pltpu.VMEM((channels, (own + 1) * LANES), jnp.bfloat16),
            pltpu.VMEM((1, channels), jnp.float32),
            pltpu.VMEM(local_delays.shape, jnp.int32),
            pltpu.VMEM(cross_delays.shape, jnp.int32),
            pltpu.VMEM((channels, (own + 1) * LANES), jnp.float32),
            pltpu.VMEM((local_levels, channels, LANES), jnp.int32),
            pltpu.VMEM((far,) + cross_delays.shape, jnp.int32),
            pltpu.VMEM((channels, frame * LANES), jnp.float32),
            pltpu.VMEM((trials, edges), jnp.int16),
            pltpu.VMEM((most + 1, trials, edges + LANES), jnp.int16),
            pltpu.VMEM((len(phases), trials, width), jnp.int16),
            pltpu.VMEM((len(phases), most, trials, width), jnp.int16),
            pltpu.SemaphoreType.DMA((4,)),
            pltpu.SemaphoreType.DMA((most + 1,)),
            pltpu.SemaphoreType.DMA((most + 1,)),
            pltpu.SemaphoreType.DMA((far,)),
            pltpu.SemaphoreType.DMA((far,)),
            pltpu.SemaphoreType.DMA((len(phases), most)),
            pltpu.SemaphoreType.DMA((len(phases), most)),
        ],
        compiler_params=pltpu.CompilerParams(collective_id=0, has_side_effects=True),
    )(filterbank, bandpass.reshape(1, channels), local_delays, cross_delays)


def solution(mesh):
    return jax.shard_map(
        shards,
        mesh=mesh,
        in_specs=(P(("beam", "sub"), "tm"), P(("beam", "sub")), P(None, "sub"), P(None, "sub")),
        out_specs=P(("beam", "sub"), "tm"),
        check_vma=False,
    )
```

```python
import functools
import math

import jax
import jax.numpy as jnp
from jax import lax
from jax.experimental import pallas as pl
from jax.experimental.pallas import tpu as pltpu
from jax.sharding import PartitionSpec as P

MESH = pl.DeviceIdType.MESH
LANES = 128
SUB = 8
HALF = 15
WINDOW = 31.0
HEADER = 32
RADIX_LEVELS = 3
TOP = 32767.0
ROUNDER = 12582912.0
TINY = 1e-30


def tiles_of(columns):
    return -(-columns // LANES)


def delayed(tiles, delay, lane, count):
    tiles = tiles[max(0, len(tiles) - count - 1) :]
    source = (lane - delay) & (LANES - 1)
    keep = lane >= delay
    turned = [jnp.take_along_axis(t, source, axis=1, mode="promise_in_bounds") for t in tiles]
    if len(turned) == count:
        turned = [jnp.zeros_like(turned[0])] + turned
    return [jnp.where(keep, turned[k + 1], turned[k]) for k in range(count)]


def merged_right(lower, upper, delay, lane, count):
    source = (lane - delay) & (LANES - 1)
    keep = lane >= delay
    turned = [jnp.take_along_axis(t, source, axis=1, mode="promise_in_bounds") for t in upper]
    zero = jnp.zeros_like(turned[0])
    made = []
    for k in range(count):
        here = turned[k] if k < len(turned) else zero
        left = turned[k - 1] if k else zero
        moved = jnp.where(keep, here, left)
        made.append(lower[k] + moved if k < len(lower) else moved)
    return made


def paired(mine, theirs, on_top, delay, lane, count):
    lower = [jnp.where(on_top, t, m) for t, m in zip(theirs, mine)]
    upper = [jnp.where(on_top, m, t) for t, m in zip(theirs, mine)]
    moved = delayed(upper, delay, lane, count)
    return [a + b for a, b in zip(lower[len(lower) - count :], moved)]


def phases_of(cross_levels):
    phases = []
    for level in range(0, cross_levels, RADIX_LEVELS):
        depth = min(RADIX_LEVELS, cross_levels - level)
        phases.append((level, depth, [m << level for m in range(1, 1 << depth)]))
    return phases


def coded(x, inverse):
    return jnp.clip(x * inverse + ROUNDER - ROUNDER, -TOP, TOP)


def scales_of(peaks):
    exponents = []
    for peak in peaks:
        top = jnp.maximum(jnp.max(peak, axis=1, keepdims=True), TINY)
        exponent = jnp.floor(jnp.log2(top) + 0.001) - 14.0
        exponents.append(jnp.broadcast_to(exponent, (SUB, LANES)))
    return exponents, [jnp.exp2(-e) for e in exponents]


def peaks_of(rows):
    return [functools.reduce(jnp.maximum, [jnp.abs(t) for t in tiles]) for tiles in rows]


def kernel(
    geometry,
    fb_hbm, bp_hbm, ld_hbm, cd_hbm,
    out_ref,
    fpad, bp_v, ld_v, cd_v, x0, delay_l, cd_far, plane, edge_sent, edge_got, sent, got,
    load_sem, edge_send, edge_recv, far_send, far_recv, cross_send, cross_recv,
):
    channels, span, local_levels, cross_levels, trials, shift_max, norm = geometry
    own = span // LANES
    before = tiles_of(cross_levels * shift_max + HEADER)
    width = before + own
    growth = trials.bit_length() - 1
    row_tiles = trials // SUB
    tm = lax.axis_index("tm")
    sub = lax.axis_index("sub")
    other = 1 - tm
    phases = phases_of(cross_levels)
    edge_masks = [0] + phases[0][2]

    counts = [tiles_of(span + HALF + (m + 1) * shift_max) for m in range(local_levels)]
    start = own + 1
    loads = [
        pltpu.make_async_copy(ld_hbm, ld_v, load_sem.at[0]),
        pltpu.make_async_copy(cd_hbm, cd_v, load_sem.at[1]),
        pltpu.make_async_copy(bp_hbm, bp_v, load_sem.at[2]),
        pltpu.make_async_copy(
            fb_hbm, fpad.at[:, pl.ds(pl.multiple_of(tm * LANES, LANES), span)], load_sem.at[3]
        ),
    ]
    for load in loads:
        load.start()

    barrier = pltpu.get_barrier_semaphore()
    partners = 0
    for mask in edge_masks:
        target = {"sub": sub ^ mask, "tm": other} if mask else {"tm": other}
        pl.semaphore_signal(barrier, inc=1, device_id=target, device_id_type=MESH)
        partners += 1
    for level, depth, masks in phases:
        for mask in masks:
            pl.semaphore_signal(barrier, inc=1, device_id={"sub": sub ^ mask}, device_id_type=MESH)
            partners += 1

    edge_tiles = counts[-1] - own + before

    @pl.when(tm == 0)
    def _():
        fpad[:, span : start * LANES] = jnp.zeros((channels, LANES), fpad.dtype)
        for slot in range(len(edge_masks)):
            edge_got[slot, :, : edge_tiles * LANES] = jnp.zeros((trials, edge_tiles * LANES), edge_got.dtype)

    @pl.when(tm == 1)
    def _():
        fpad[:, :LANES] = jnp.zeros((channels, LANES), fpad.dtype)
        for slot in range(len(edge_masks)):
            edge_got[slot, :, edge_tiles * LANES :] = jnp.zeros((trials, LANES), edge_got.dtype)

    for load in loads[:3]:
        load.wait()
    ones = jnp.ones((channels, LANES), jnp.float32).astype(jnp.bfloat16)
    row_at = lax.broadcasted_iota(jnp.int32, (channels, channels), 0)
    col_at = lax.broadcasted_iota(jnp.int32, (channels, channels), 1)
    diagonal = row_at == col_at
    rows = channels
    for level in range(local_levels):
        if level >= growth:
            rows //= 2
        spread = jnp.where(diagonal[:rows], ld_v[level : level + 1, :].astype(jnp.float32), 0.0)
        spread = jnp.dot(spread.astype(jnp.bfloat16), ones, preferred_element_type=jnp.float32)
        delay_l[level, :rows, :] = spread.astype(jnp.int32)

    def spread_of(delays):
        spread = jnp.where(diagonal[:trials, :trials], delays.astype(jnp.float32), 0.0)
        spread = jnp.dot(spread.astype(jnp.bfloat16), ones[:trials], preferred_element_type=jnp.float32)
        return spread.astype(jnp.int32)

    delay_c = [spread_of(cd_v[level : level + 1, :]) for level in range(cross_levels)]
    gain = jnp.dot(
        jnp.where(diagonal, bp_v[...], 0.0), jnp.ones((channels, LANES), jnp.float32),
        precision=lax.Precision.HIGHEST, preferred_element_type=jnp.float32,
    )
    band_row = lax.broadcasted_iota(jnp.int32, (3 * LANES, LANES), 0)
    band_col = lax.broadcasted_iota(jnp.int32, (3 * LANES, LANES), 1)
    apart = band_row - LANES - band_col
    band = jnp.where((apart >= -HALF) & (apart <= HALF), 1.0, 0.0).astype(jnp.bfloat16)

    loads[3].wait()
    for k in range(start):
        low, high = max(k - 1, 0), min(k + 2, start)
        total = jnp.dot(
            fpad[:, low * LANES : high * LANES], band[(low - k + 1) * LANES : (high - k + 1) * LANES],
            preferred_element_type=jnp.float32,
        )
        centre = fpad[:, k * LANES : (k + 1) * LANES].astype(jnp.float32)
        x0[:, k * LANES : (k + 1) * LANES] = gain * (centre - total / WINDOW)

    lane = lax.broadcasted_iota(jnp.int32, (SUB, LANES), 1)
    sublane = lax.broadcasted_iota(jnp.int32, (SUB, LANES), 0)

    def block(at, carry):
        base = at * trials
        current = []
        for r in range(row_tiles):
            here = pl.ds(pl.multiple_of(base + r * SUB, SUB), SUB)
            current.append([x0[here, k * LANES : (k + 1) * LANES] for k in range(start)])
        for level in range(growth):
            count, step = counts[level], 1 << level
            following = []
            for r in range(row_tiles):
                delay = delay_l[level, pl.ds(pl.multiple_of(base + r * SUB, SUB), SUB), :]
                if step < SUB:
                    is_upper = (sublane & step) != 0
                    lower, upper = [], []
                    for t in current[r]:
                        down = pltpu.roll(t, step, 0)
                        up = down if 2 * step == SUB else pltpu.roll(t, SUB - step, 0)
                        lower.append(jnp.where(is_upper, down, t))
                        upper.append(jnp.where(is_upper, t, up))
                else:
                    apart = step // SUB
                    lower, upper = current[r & ~apart], current[r | apart]
                following.append(merged_right(lower, upper, delay, lane, count))
            current = following
        for r in range(row_tiles):
            here = pl.ds(pl.multiple_of(base + r * SUB, SUB), SUB)
            for k, t in enumerate(current[r]):
                plane[here, k * LANES : (k + 1) * LANES] = t
        return carry

    lax.fori_loop(0, channels // trials, block, 0, unroll=True)

    bands = channels // trials
    count = counts[growth - 1]
    current = [
        [[plane[(b * row_tiles + r) * SUB : (b * row_tiles + r + 1) * SUB, k * LANES : (k + 1) * LANES] for k in range(count)] for r in range(row_tiles)]
        for b in range(bands)
    ]
    for level in range(growth, local_levels):
        count = counts[level]
        bands //= 2
        following = []
        for b in range(bands):
            made = []
            for r in range(row_tiles):
                at = (b * row_tiles + r) * SUB
                delay = delay_l[level, at : at + SUB, :]
                made.append(merged_right(current[2 * b][r], current[2 * b + 1][r], delay, lane, count))
            following.append(made)
        current = following
    frame = current[0]


    rows_of = []
    for r in range(row_tiles):
        tiles = []
        for t in range(-before, own):
            zero = jnp.zeros_like(frame[r][0])
            early = frame[r][t] if t >= 0 else zero
            late = frame[r][t + 1] if t >= -1 else zero
            tiles.append(jnp.where(tm == 1, late, early))
        rows_of.append(tiles)

    wide_lane = lax.broadcasted_iota(jnp.int32, (trials, LANES), 1)
    is_header = wide_lane < HEADER

    def fill(ref, k, tiles, inverses, header):
        if tiles is None:
            tile = header
        else:
            tile = jnp.concatenate([coded(t, i) for t, i in zip(tiles, inverses)], axis=0)
            if header is not None:
                tile = jnp.where(is_header, header, tile)
        ref[:, k * LANES : (k + 1) * LANES] = tile.astype(jnp.int32).astype(jnp.int16)

    def prepare(at, rows, exponents, inverses):
        header = jnp.concatenate(exponents, axis=0)
        skip = width - len(rows[0])
        for k in range(width):
            if k == 0 or k >= skip:
                fill(sent.at[at], k, [p[k - skip] for p in rows] if k >= skip else None, inverses, None if k else header)

    def plane_copy(at, index, mask):
        return pltpu.make_async_remote_copy(
            src_ref=sent.at[at], dst_ref=got.at[at, index],
            send_sem=cross_send.at[at, index], recv_sem=cross_recv.at[at, index],
            device_id={"sub": sub ^ mask}, device_id_type=MESH,
        )

    def edge_pair(slot, mask):
        target = {"tm": other} if isinstance(mask, int) and mask == 0 else {"sub": sub ^ mask, "tm": other}
        onward = pltpu.make_async_remote_copy(
            src_ref=edge_sent, dst_ref=edge_got.at[slot, :, pl.ds(0, edge_tiles * LANES)],
            send_sem=edge_send.at[slot], recv_sem=edge_recv.at[slot],
            device_id=target, device_id_type=MESH,
        )
        backward = pltpu.make_async_remote_copy(
            src_ref=edge_sent.at[:, pl.ds(0, LANES)], dst_ref=edge_got.at[slot, :, pl.ds(edge_tiles * LANES, LANES)],
            send_sem=edge_send.at[slot], recv_sem=edge_recv.at[slot],
            device_id=target, device_id_type=MESH,
        )
        return onward, backward

    far_copies = {}
    for level, depth, masks in phases:
        for mask in masks[1::2]:
            index = len(far_copies)
            far_copies[mask] = pltpu.make_async_remote_copy(
                src_ref=cd_v, dst_ref=cd_far.at[index],
                send_sem=far_send.at[index], recv_sem=far_recv.at[index],
                device_id={"sub": sub ^ mask}, device_id_type=MESH,
            )
    far_at = {mask: index for index, mask in enumerate(far_copies)}
    plane_copies = [[plane_copy(at, index, mask) for index, mask in enumerate(masks)] for at, (_, _, masks) in enumerate(phases)]
    edge_copies = [edge_pair(slot, mask) for slot, mask in enumerate(edge_masks)]

    exponents, inverses = scales_of(peaks_of(frame))
    prepare(0, rows_of, exponents, inverses)
    header = jnp.concatenate(exponents, axis=0)
    for k in range(edge_tiles):
        onward = [frame[r][own - before + k] for r in range(row_tiles)]
        if k == 0:
            onward = [jnp.where(tm == 1, frame[r][0], onward[r]) for r in range(row_tiles)]
        fill(edge_sent, k, onward, inverses, None if k else header)

    pl.semaphore_wait(barrier, partners)
    for copy in far_copies.values():
        copy.start()

    low = sub & 1
    pairs = len(edge_masks) // 2
    mine_at = (sub >> 1) & (pairs - 1)
    for pair in list(range(1, pairs)) + [0]:
        for turn in (0, 1):
            if pair:
                receiver = pair - 1 + (mine_at < pair).astype(jnp.int32)
                slot = 2 * (receiver ^ mine_at) + (turn ^ low)
                plane_copy(0, slot - 1, slot).start()
            elif turn == 0:
                plane_copies[0][0].start()
            first, second = edge_pair(slot, slot) if pair else edge_copies[turn]

            @pl.when(tm == 0)
            def _():
                first.start()

            @pl.when(tm == 1)
            def _():
                second.start()

    def decoded(tile):
        return tile.astype(jnp.int32).astype(jnp.float32)

    def split(tile):
        return [tile[r * SUB : (r + 1) * SUB] for r in range(row_tiles)]

    def scale_from(header):
        return jnp.exp2(jnp.broadcast_to(header[:, :1], (trials, LANES)))

    def wait_edges(slots):
        @pl.when(tm == 0)
        def _():
            for slot in slots:
                edge_copies[slot][1].wait_recv()

        @pl.when(tm == 1)
        def _():
            for slot in slots:
                edge_copies[slot][0].wait_recv()

    def with_edge(slot, rows):
        tiles = [decoded(edge_got[slot, :, k * LANES : (k + 1) * LANES]) for k in range(edge_tiles + 1)]
        scale = scale_from(jnp.where(tm == 1, tiles[0], tiles[-1]))
        tiles[-1] = jnp.where(is_header, 0.0, tiles[-1])
        made = [list(row) for row in rows]
        for at, tile in zip(list(range(edge_tiles)) + [width - 1], tiles):
            for r, part in enumerate(split(tile * scale)):
                made[r][at] = made[r][at] + part
        return made

    def wait_for(at, wanted):
        for mask in wanted:
            if mask:
                plane_copies[at][phases[at][2].index(mask)].wait_recv()
        if at == 0:
            wait_edges(wanted)

    def landed(at, mask, count):
        if mask == 0:
            rows = rows_of
        else:
            index = phases[at][2].index(mask)
            tiles = [decoded(got[at, index, :, k * LANES : (k + 1) * LANES]) for k in [0] + list(range(max(width - count, 1), width))]
            scale = scale_from(tiles[0])
            tiles = tiles[1:] if count < width else tiles
            parts = [split(t * scale) for t in tiles]
            rows = [[p[r] for p in parts] for r in range(row_tiles)]
        return rows if at else with_edge(edge_masks.index(mask), rows)

    def merged(at, mask, depth):
        step = phases[at][0] + depth - 1
        count = own + tiles_of((cross_levels - step - 1) * shift_max)
        upper = mask | (1 << step)
        if depth == 1:
            wait_for(at, [mask, upper])
            mine, theirs = [landed(at, m, len(rows_of[0])) for m in (mask, upper)]
        else:
            mine, theirs = [merged(at, m, depth - 1) for m in (mask, upper)]
        delay = delay_c[step] if mask == 0 else delay_far[mask, step]
        on_top = (sub >> step) & 1 == 1
        return [paired(mine[r], theirs[r], on_top, delay[r * SUB : (r + 1) * SUB], lane, count) for r in range(row_tiles)]

    for at, (level, depth, masks) in enumerate(phases):
        if at:
            prepare(at, rows_of, *scales_of(peaks_of(rows_of)))
            for copy in reversed(plane_copies[at]):
                copy.start()
        delay_far = {}
        for mask in masks[1::2]:
            far_copies[mask].wait_recv()
        for mask in masks[1::2]:
            for step in range(level, level + depth - 1):
                if (mask >> level) % (2 << (step - level)) == 0:
                    delay_far[mask, step] = spread_of(cd_far[far_at[mask], step : step + 1, :])
        rows_of = merged(at, 0, depth)

    for r in range(row_tiles):
        for k, t in enumerate(rows_of[r][-own:]):
            out_ref[r * SUB : (r + 1) * SUB, k * LANES : (k + 1) * LANES] = t * norm
    for copy in [c for row in plane_copies for c in row] + list(far_copies.values()):
        copy.wait_send()

    @pl.when(tm == 0)
    def _():
        for onward, backward in edge_copies:
            onward.wait_send()

    @pl.when(tm == 1)
    def _():
        for onward, backward in edge_copies:
            backward.wait_send()


def shards(filterbank, bandpass, local_delays, cross_delays):
    channels, span = filterbank.shape
    shift_max = span // 16
    local_levels = local_delays.shape[0]
    cross_levels = lax.axis_size("sub").bit_length() - 1
    trials = cross_delays.shape[1]
    norm = 1.0 / math.sqrt(channels * lax.axis_size("sub"))
    own = span // LANES
    before = tiles_of(cross_levels * shift_max + HEADER)
    width = (own + before) * LANES
    frame = tiles_of(span + HALF + local_levels * shift_max)
    edges = (frame - own + before) * LANES
    phases = phases_of(cross_levels)
    most = len(phases[0][2])
    far = max(sum(len(masks[1::2]) for _, _, masks in phases), 1)
    geometry = (channels, span, local_levels, cross_levels, trials, shift_max, norm)
    return pl.pallas_call(
        functools.partial(kernel, geometry),
        out_shape=pltpu.VMEM((trials, span), jnp.float32),
        in_specs=[pl.BlockSpec(memory_space=pl.ANY)] * 4,
        out_specs=pl.BlockSpec(memory_space=pltpu.VMEM),
        scratch_shapes=[
            pltpu.VMEM((channels, (own + 1) * LANES), jnp.bfloat16),
            pltpu.VMEM((1, channels), jnp.float32),
            pltpu.VMEM(local_delays.shape, jnp.int32),
            pltpu.VMEM(cross_delays.shape, jnp.int32),
            pltpu.VMEM((channels, (own + 1) * LANES), jnp.float32),
            pltpu.VMEM((local_levels, channels, LANES), jnp.int32),
            pltpu.VMEM((far,) + cross_delays.shape, jnp.int32),
            pltpu.VMEM((channels, frame * LANES), jnp.float32),
            pltpu.VMEM((trials, edges), jnp.int16),
            pltpu.VMEM((most + 1, trials, edges + LANES), jnp.int16),
            pltpu.VMEM((len(phases), trials, width), jnp.int16),
            pltpu.VMEM((len(phases), most, trials, width), jnp.int16),
            pltpu.SemaphoreType.DMA((4,)),
            pltpu.SemaphoreType.DMA((most + 1,)),
            pltpu.SemaphoreType.DMA((most + 1,)),
            pltpu.SemaphoreType.DMA((far,)),
            pltpu.SemaphoreType.DMA((far,)),
            pltpu.SemaphoreType.DMA((len(phases), most)),
            pltpu.SemaphoreType.DMA((len(phases), most)),
        ],
        compiler_params=pltpu.CompilerParams(collective_id=0, has_side_effects=True),
    )(filterbank, bandpass.reshape(1, channels), local_delays, cross_delays)


def solution(mesh):
    return jax.shard_map(
        shards,
        mesh=mesh,
        in_specs=(P(("beam", "sub"), "tm"), P(("beam", "sub")), P(None, "sub"), P(None, "sub")),
        out_specs=P(("beam", "sub"), "tm"),
        check_vma=False,
    )
```
